32 devices in a mesh: lat: 4 (over y, x), lon: 8 (over z, core).
Axes of the slice: x: 2, y: 2, z: 4, core: 2. Of those that a mesh axis runs over, the one named last changes fastest.
Arguments:
- control: float32 [548, 32, 1024], P(None, 'lat', 'lon'), may hold values from -6 to 6
- std_dev: float32 [548], replicated, may hold values from 0.3 to 3
- col_dev: int32 [3072, 1], P(('lat', 'lon')), may hold values from 0 to 31; in each aligned block of 96 rows (0 to 95, 96 to 191, ...) at most 6 rows name the same one
- col_cell: int32 [3072], P(('lat', 'lon')), may hold values from 0 to 1023
- jacobian: bfloat16 [3072, 150, 548], P(('lat', 'lon')), may hold values from -0.25 to 0.25
- innovation: float32 [3072, 150], P(('lat', 'lon')), may hold values from -6 to 6
- inv_error: float32 [150], replicated, may hold values from 0.3 to 3
Outputs:
- departures: float32 [3072, 150], P(('lat', 'lon'))
- increment: float32 [548, 32, 1024], P(None, 'lat', 'lon')
- adjoint: float32 [548, 32, 1024], P(None, 'lat', 'lon')
The draws below stay inside these ranges and needn't reach their ends.
Inputs may be any that keep to these rules, and one draw needn't show every extreme that they name: `col_dev`: among the soundings of one device (aligned blocks of 96 rows) at most 6 name the same device, and in every draw some device is named exactly 6 times by one block.
All inputs are finite; a program needn't handle non-finite values.
Results may differ from the reference program's by a relative error of at most 0.0025.
Values may be sent and summed in bfloat16 or wider, within the bound.
A program may use at most 128 MiB of HBM per device.

```python
import math
import jax
import jax.numpy as jnp
import numpy as np
from jax import lax

COL = 548
CH = 150
TLAT = 8
TLON = 128
LHALF = 8
S_DEV = 96
CAP = 6
NLAT = 32
NLON = 1024
SOUND = 3072
N_LAT = 4
N_LON = 8
DEVICES = 32


def place_ends(result, stream_key, low, top_value):
    shape = result.shape
    index_at = [jax.random.randint(jax.random.fold_in(stream_key, axis), (), 0, shape[axis]) for axis in range(len(shape))]
    result = result.at[tuple(index_at)].set(low)
    longest = shape.index(max(shape))
    index_at[longest] = (index_at[longest] + 1) % shape[longest]
    return result.at[tuple(index_at)].set(top_value)


def levels(stream_key, dims, pieces, low, largest):
    level, own = 1.0, jax.random.fold_in(stream_key, 6)
    for axis_at, shards_of in pieces:
        steps = jnp.exp(jax.random.uniform(jax.random.fold_in(own, axis_at), (shards_of,), jnp.float32, low / len(pieces), largest / len(pieces)))
        level = level * jnp.repeat(steps, dims[axis_at] // shards_of).reshape([-1 if axis == axis_at else 1 for axis in range(len(dims))])
    return level


def routed_block(rng, own, number, rows, amount, top, most, lean):
    ranking = jax.random.permutation(rng, amount)
    packed, ordinary = shares(amount, rows * top, most, lean, True), shares(amount, rows * top, most, lean, False)
    places = jnp.arange(amount)

    def named(tallies, rotation):
        used = int((tallies > 0).sum())
        fixed = max(1, used // 4)
        shifted = fixed + (places - fixed + rotation * (used - fixed)) % max(1, amount - fixed)
        return jnp.zeros((amount,), jnp.int32).at[ranking[jnp.where(places < fixed, places, shifted)]].set(jnp.asarray(tallies, jnp.int32))

    tallies = jnp.where(number % 4 == 0, named(packed, number // 4), named(ordinary, number - number // 4 - 1))
    mixed = jax.random.permutation(jax.random.fold_in(own, 3), amount)
    giver, receiver = mixed[0:amount // 2 * 2:2], mixed[1:amount // 2 * 2:2]
    margin = jnp.minimum(tallies[giver] - 1, most - tallies[receiver]) // 2
    margin = jnp.where((giver == ranking[0]) | (receiver == ranking[0]) | (tallies[receiver] == 0), 0, jnp.maximum(margin, 0))
    shifted = jax.random.randint(jax.random.fold_in(own, 4), (amount // 2,), 0, 1 << 20) % (margin + 1)
    tallies = tallies.at[giver].add(-shifted).at[receiver].add(shifted)
    items = jnp.searchsorted(jnp.cumsum(tallies), jnp.arange(rows * top), side="right").astype(jnp.int32)
    listing = items.reshape(top, rows).T
    listing = listing[jax.random.permutation(jax.random.fold_in(own, 1), rows)]
    rotation = jax.random.randint(jax.random.fold_in(own, 2), (rows, 1), 0, top)
    return jnp.take_along_axis(listing, (jnp.arange(top)[None, :] + rotation) % top, axis=1)


def shares(number_of, total, limit, skew, full):
    portions = [(1 << 20) // math.isqrt(standing ** skew) + 1 for standing in range(1, number_of + 1)]
    largest = limit if full else min(limit, max(-(-total // number_of), total * portions[0] // sum(portions)))
    least = 1 if total - largest >= number_of - 1 else 0
    holding, rest = [largest] + [least] * (number_of - 1), total - largest - least * (number_of - 1)
    while rest > 0:
        free = [i for i in range(1, number_of) if holding[i] < largest] or [i for i in range(1, number_of) if holding[i] < limit]
        pool, left = sum([portions[i] for i in free]), rest
        for i in free:
            more = min(limit - holding[i], max(1, left * portions[i] // pool), rest)
            holding[i] = holding[i] + more
            rest = rest - more
    return np.array(holding)


def noise(key, dims, scale, reach, pieces=(), kind=jnp.bfloat16):
    loudness = levels(key, dims, pieces, -0.22, 0.18) if pieces else 1.0
    array = jax.random.normal(key, dims, jnp.float32) * scale * loudness
    return jnp.minimum(jnp.maximum(array, -reach), reach).astype(kind)


def setup_inputs(seed: int = 0) -> dict:
    arg_keys = jax.random.split(jax.random.key(seed), 8)
    control = noise(arg_keys[0], (COL, NLAT, NLON), 1.0, 6.0, ((1, 4), (2, 8)), jnp.float32)
    std_dev = jnp.clip(jnp.exp(jax.random.uniform(arg_keys[1], (COL,), jnp.float32, math.log(0.3), math.log(3.0))), 0.3, 3.0)
    col_dev_keys = jax.random.split(jax.random.fold_in(arg_keys[2], 1), SOUND // S_DEV)
    col_dev_turns = jax.random.permutation(jax.random.fold_in(arg_keys[2], 3), SOUND // S_DEV)
    col_dev = jax.vmap(lambda own, number: routed_block(jax.random.fold_in(arg_keys[2], 2), own, number, S_DEV, DEVICES, 1, CAP, 2))(col_dev_keys, col_dev_turns).reshape((SOUND, 1))
    col_cell = place_ends(jax.random.randint(arg_keys[3], (SOUND,), 0, TLAT * TLON), jax.random.fold_in(arg_keys[3], 1), 0, (TLAT * TLON) - 1).astype(jnp.int32)
    jacobian = noise(arg_keys[4], (SOUND, CH, COL), COL ** -0.5, 0.25, ((0, 32),))
    innovation = noise(arg_keys[5], (SOUND, CH), 1.0, 6.0, ((0, 32),), jnp.float32)
    inv_error = jnp.clip(jnp.exp(jax.random.uniform(arg_keys[6], (CH,), jnp.float32, math.log(0.3), math.log(3.0))), 0.3, 3.0)
    return {"control": control, "std_dev": std_dev, "col_dev": col_dev, "col_cell": col_cell, "jacobian": jacobian, "innovation": innovation, "inv_error": inv_error}


def band(out_count, in_count, half_width):
    row_index = jnp.arange(out_count, dtype=jnp.int32)[:, None]
    col_index = jnp.arange(in_count, dtype=jnp.int32)[None, :]
    offset = (col_index - row_index - half_width).astype(jnp.float32)
    spread = 2.0 * half_width / 3.0
    taps = jnp.arange(-half_width, half_width + 1, dtype=jnp.int32).astype(jnp.float32)
    norm_total = jnp.sqrt(jnp.sum(jnp.exp(-taps * taps / (spread * spread))))
    weights = jnp.exp(-offset * offset / (2.0 * spread * spread)) / norm_total
    return jnp.where(jnp.abs(offset) <= half_width, weights, jnp.zeros_like(weights))

def along_lat(grid_field):
    half_width = LHALF
    extended = jnp.pad(grid_field, ((0, 0), (half_width, half_width), (0, 0)))
    lat_band = band(TLAT, TLAT + 2 * half_width, half_width)

    def one_block(block):
        window = lax.dynamic_slice_in_dim(extended, block * TLAT, TLAT + 2 * half_width, 1)
        return jnp.einsum('ij,cjk->cik', lat_band, window, precision=lax.Precision.HIGHEST)
    blocks = lax.map(one_block, jnp.arange(N_LAT, dtype=jnp.int32))
    return jnp.transpose(blocks, (1, 0, 2, 3)).reshape(grid_field.shape)

def along_lon(grid_field):
    half_width = TLON // 2
    extended = jnp.concatenate([grid_field[:, :, -half_width:], grid_field, grid_field[:, :, :half_width]], axis=2)
    lon_band = band(TLON, TLON + 2 * half_width, half_width)

    def one_block(block):
        window = lax.dynamic_slice_in_dim(extended, block * TLON, TLON + 2 * half_width, 2)
        return jnp.einsum('cik,jk->cij', window, lon_band, precision=lax.Precision.HIGHEST)
    blocks = lax.map(one_block, jnp.arange(N_LON, dtype=jnp.int32))
    return jnp.transpose(blocks, (1, 2, 0, 3)).reshape(grid_field.shape)

def reference(control, std_dev, col_dev, col_cell, jacobian, innovation, inv_error):
    width, lat_rows, lon_cols = control.shape
    increment = along_lon(along_lat(control)) * std_dev[:, None, None]
    target = col_dev[:, 0]
    row_of = target // N_LON * TLAT + col_cell // TLON
    column_of = target % N_LON * TLON + col_cell % TLON
    columns = increment[:, row_of, column_of].T.astype(jnp.bfloat16)

    def per_device(items):
        jac_block, col_block, innov_block = items
        jac_wide = jac_block.astype(jnp.float32)
        evolved = jnp.einsum('sqc,sc->sq', jac_wide, col_block.astype(jnp.float32))
        deps = evolved - innov_block
        weighted = (deps * inv_error[None, :]).astype(jnp.bfloat16)
        column_grad = jnp.einsum('sqc,sq->sc', jac_wide, weighted.astype(jnp.float32))
        return (deps, column_grad)
    departures, column_grad = lax.map(per_device, (jacobian.reshape(DEVICES, S_DEV, CH, width), columns.reshape(DEVICES, S_DEV, width), innovation.reshape(DEVICES, S_DEV, CH)))
    departures = departures.reshape(SOUND, CH)
    column_grad = column_grad.reshape(SOUND, width)
    flat_index = (row_of * lon_cols + column_of).astype(jnp.int32)
    gathered = jnp.zeros((width, lat_rows * lon_cols), jnp.float32).at[:, flat_index].add(column_grad.T)
    gathered = gathered.reshape(width, lat_rows, lon_cols) * std_dev[:, None, None]
    adjoint = along_lat(along_lon(gathered))
    return (departures, increment, adjoint)
```

```python
import jax
import jax.numpy as jnp
from jax import lax
from jax.sharding import PartitionSpec as P

LHALF = 8
HIGHEST = lax.Precision.HIGHEST


def tap_weights(offset, half_width):
    spread = 2.0 * half_width / 3.0
    taps = jnp.arange(-half_width, half_width + 1, dtype=jnp.int32).astype(jnp.float32)
    norm_total = jnp.sqrt(jnp.sum(jnp.exp(-taps * taps / (spread * spread))))
    weights = jnp.exp(-offset * offset / (2.0 * spread * spread)) / norm_total
    return jnp.where(jnp.abs(offset) <= half_width, weights, jnp.zeros_like(weights))


def band(out_count, in_count, half_width):
    row_index = jnp.arange(out_count, dtype=jnp.int32)[:, None]
    col_index = jnp.arange(in_count, dtype=jnp.int32)[None, :]
    return tap_weights((col_index - row_index - half_width).astype(jnp.float32), half_width)


def shifts(axis, wrap):
    peers = lax.axis_size(axis)
    up = [(i, (i + 1) % peers) for i in range(peers if wrap else peers - 1)]
    return up, [(j, i) for i, j in up]


def around(array, axis, wrap):
    up, down = shifts(axis, wrap)
    return lax.ppermute(array, axis, up), lax.ppermute(array, axis, down)


def halves(weights):
    high = weights.astype(jnp.bfloat16)
    return high, (weights - high.astype(jnp.float32)).astype(jnp.bfloat16)


def dot_split(data, weights):
    high, low = halves(weights)
    dot = lambda w: jnp.dot(data, w, preferred_element_type=jnp.float32)
    return dot(high) + dot(low)


def smooth(field, before, after):
    width, lat_rows, lon_cols = field.shape
    extended = jnp.concatenate([before.astype(jnp.float32), field, after.astype(jnp.float32)], axis=1)
    lat_band = band(lat_rows, lat_rows + 2 * LHALF, LHALF)
    field = jnp.einsum("ij,cjk->cik", lat_band, extended, precision=HIGHEST)
    lon_half, part = lon_cols // 2, width // 2
    rounded = field.astype(jnp.bfloat16)
    paired = lambda piece: jnp.concatenate([piece[:part], piece[part:]], axis=2)
    up, down = shifts("lon", True)
    left = lax.ppermute(paired(rounded[:, :, lon_half:]), "lon", up)
    right = lax.ppermute(paired(rounded[:, :, :lon_half]), "lon", down)
    lon_band = band(lon_cols, lon_cols + 2 * lon_half, lon_half).T
    edge = lambda w: jnp.concatenate(
        [jnp.concatenate([w, jnp.zeros_like(w)], 1), jnp.concatenate([jnp.zeros_like(w), w], 1)], 0
    )
    both = jnp.concatenate([left, right], axis=2).reshape(part * lat_rows, 2 * lon_cols)
    weights = jnp.concatenate([edge(lon_band[:lon_half]), edge(lon_band[-lon_half:])], 0)
    sides = dot_split(both, weights)
    sides = jnp.concatenate([sides[:, :lon_cols], sides[:, lon_cols:]], axis=0)
    own = jnp.dot(
        field.reshape(width * lat_rows, lon_cols), lon_band[lon_half:-lon_half], precision=HIGHEST
    )
    return (own + sides).reshape(width, lat_rows, lon_cols)


def local(control, std_dev, col_dev, col_cell, jacobian, innovation, inv_error):
    width, lat_rows, lon_cols = control.shape
    devices = lax.axis_size("lat") * lax.axis_size("lon")
    sound_count = col_cell.shape[0]
    slots_each = max(2, 2 * sound_count // devices)
    slots = devices * slots_each

    before, after = around(control.astype(jnp.bfloat16), "lat", False)

    target = col_dev[:, 0]
    onehot = (target[:, None] == jnp.arange(devices, dtype=jnp.int32)[None, :]).astype(jnp.int32)
    below = jnp.arange(sound_count)[:, None] > jnp.arange(sound_count)[None, :]
    earlier = jnp.dot(
        below.astype(jnp.bfloat16), onehot.astype(jnp.bfloat16), preferred_element_type=jnp.float32
    ).astype(jnp.int32)
    order_in = jnp.sum(earlier * onehot, axis=1)
    slot = target * slots_each + order_in
    wanted = jnp.zeros((slots,), jnp.int32).at[slot].set(col_cell)
    requested = lax.all_to_all(
        wanted.reshape(devices, slots_each), ("lat", "lon"), split_axis=0, concat_axis=0, tiled=True
    ).reshape(-1)

    cells = jnp.stack([requested, *around(requested, "lat", False)])
    cells = jnp.stack([cells, *around(cells, "lon", True)]).reshape(3, 3, slots)
    shift = jnp.array([0, -1, 1], jnp.int32)
    rows = (cells // lon_cols + lat_rows * shift[None, :, None]).reshape(-1, 1)
    columns_at = (cells % lon_cols + lon_cols * shift[:, None, None]).reshape(-1, 1)
    row_weight = tap_weights((rows - jnp.arange(lat_rows)[None, :]).astype(jnp.float32), LHALF)
    col_weight = tap_weights((columns_at - jnp.arange(lon_cols)[None, :]).astype(jnp.float32), lon_cols // 2)
    spread = (row_weight[:, :, None] * col_weight[:, None, :]).reshape(-1, lat_rows * lon_cols)
    spread_high, spread_low = halves(spread)

    increment = smooth(control, before, after) * std_dev[:, None, None]
    flat_field = increment.reshape(width, lat_rows * lon_cols)
    picked = jnp.take(flat_field, requested, axis=1).T.astype(jnp.bfloat16)
    returned = lax.all_to_all(
        picked.reshape(devices, slots_each, width), ("lat", "lon"), split_axis=0, concat_axis=0, tiled=True
    )
    columns = returned.reshape(slots, width)[slot]
    evolved = jnp.einsum("sqc,sc->sq", jacobian, columns, preferred_element_type=jnp.float32)
    departures = evolved - innovation
    weighted = (departures * inv_error[None, :]).astype(jnp.bfloat16)
    column_grad = jnp.einsum("sqc,sq->sc", jacobian, weighted, preferred_element_type=jnp.float32)
    outgoing = jnp.zeros((slots, width), jnp.bfloat16).at[slot].set(column_grad.astype(jnp.bfloat16))
    arrived = lax.all_to_all(
        outgoing.reshape(devices, slots_each, width), ("lat", "lon"), split_axis=0, concat_axis=0, tiled=True
    ).reshape(slots, width)
    near = jnp.concatenate([arrived, *around(arrived, "lat", False)], axis=0)
    near = jnp.concatenate([near, *around(near, "lon", True)], axis=0)
    add_up = lambda w: lax.dot_general(
        near, w, (((0,), (0,)), ((), ())), preferred_element_type=jnp.float32
    )
    adjoint = (add_up(spread_high) + add_up(spread_low)) * std_dev[:, None]
    return (departures, increment, adjoint.reshape(width, lat_rows, lon_cols))


def solution(mesh):
    placed = (
        P(None, "lat", "lon"),
        P(),
        P(("lat", "lon"), None),
        P(("lat", "lon")),
        P(("lat", "lon"), None, None),
        P(("lat", "lon"), None),
        P(),
    )
    return jax.shard_map(
        local,
        mesh=mesh,
        in_specs=placed,
        out_specs=(P(("lat", "lon"), None), P(None, "lat", "lon"), P(None, "lat", "lon")),
        check_vma=False,
    )
```

```python
import functools

import jax
import jax.numpy as jnp
from jax import lax
from jax.experimental import pallas as pl
from jax.experimental.pallas import tpu as pltpu
from jax.sharding import PartitionSpec as P

LHALF = 8
HIGHEST = lax.Precision.HIGHEST


def tap_weights(offset, half_width):
    spread = 2.0 * half_width / 3.0
    taps = jnp.arange(-half_width, half_width + 1, dtype=jnp.int32).astype(jnp.float32)
    norm_total = jnp.sqrt(jnp.sum(jnp.exp(-taps * taps / (spread * spread))))
    weights = jnp.exp(-offset * offset / (2.0 * spread * spread)) / norm_total
    return jnp.where(jnp.abs(offset) <= half_width, weights, jnp.zeros_like(weights))


def band(out_count, in_count, half_width):
    row_index = jnp.arange(out_count, dtype=jnp.int32)[:, None]
    col_index = jnp.arange(in_count, dtype=jnp.int32)[None, :]
    return tap_weights((col_index - row_index - half_width).astype(jnp.float32), half_width)


def shifts(axis, wrap):
    peers = lax.axis_size(axis)
    up = [(i, (i + 1) % peers) for i in range(peers if wrap else peers - 1)]
    return up, [(j, i) for i, j in up]


def around(array, axis, wrap):
    up, down = shifts(axis, wrap)
    return lax.ppermute(array, axis, up), lax.ppermute(array, axis, down)


def halves(weights):
    high = weights.astype(jnp.bfloat16)
    return high, (weights - high.astype(jnp.float32)).astype(jnp.bfloat16)


def dot_split(data, weights):
    high, low = halves(weights)
    dot = lambda w: jnp.dot(data, w, preferred_element_type=jnp.float32)
    return dot(high) + dot(low)


def smooth(field, before, after):
    width, lat_rows, lon_cols = field.shape
    extended = jnp.concatenate([before.astype(jnp.float32), field, after.astype(jnp.float32)], axis=1)
    lat_band = band(lat_rows, lat_rows + 2 * LHALF, LHALF)
    field = jnp.einsum("ij,cjk->cik", lat_band, extended, precision=HIGHEST)
    lon_half, part = lon_cols // 2, width // 2
    rounded = field.astype(jnp.bfloat16)
    paired = lambda piece: jnp.concatenate([piece[:part], piece[part:]], axis=2)
    up, down = shifts("lon", True)
    left = lax.ppermute(paired(rounded[:, :, lon_half:]), "lon", up)
    right = lax.ppermute(paired(rounded[:, :, :lon_half]), "lon", down)
    lon_band = band(lon_cols, lon_cols + 2 * lon_half, lon_half).T
    edge = lambda w: jnp.concatenate(
        [jnp.concatenate([w, jnp.zeros_like(w)], 1), jnp.concatenate([jnp.zeros_like(w), w], 1)], 0
    )
    both = jnp.concatenate([left, right], axis=2).reshape(part * lat_rows, 2 * lon_cols)
    weights = jnp.concatenate([edge(lon_band[:lon_half]), edge(lon_band[-lon_half:])], 0)
    sides = dot_split(both, weights)
    sides = jnp.concatenate([sides[:, :lon_cols], sides[:, lon_cols:]], axis=0)
    own = jnp.dot(
        field.reshape(width * lat_rows, lon_cols), lon_band[lon_half:-lon_half], precision=HIGHEST
    )
    return (own + sides).reshape(width, lat_rows, lon_cols)


def lane_tiles(count):
    return -(-count // 128)


def fold_lanes(tile):
    rows, count = tile.shape
    total = tile[:, :128]
    for start in range(128, count, 128):
        total = total + tile[:, start : start + 128]
    return total


def sounding_kernel(channels, step, jac_ref, col_ref, innov_ref, inv_ref, dep_ref, grad_ref):
    rows, width = col_ref.shape
    lanes = lax.broadcasted_iota(jnp.int32, (rows, dep_ref.shape[1]), 1)
    columns = col_ref[...].astype(jnp.float32)
    dep_ref[...] = jnp.zeros_like(dep_ref)
    grad_ref[...] = jnp.zeros_like(grad_ref)

    def some(index, carry):
        weighted = []
        found = jnp.zeros(dep_ref.shape, jnp.float32)
        for k in range(step):
            channel = index * step + k
            product = jac_ref[channel].astype(jnp.float32) * columns
            departure = jnp.sum(product, axis=1, keepdims=True)
            departure = departure - jnp.sum(
                jnp.where(lanes == channel, innov_ref[...], 0.0), axis=1, keepdims=True
            )
            found = found + jnp.where(lanes == channel, departure, 0.0)
            weight = (departure * inv_ref[0, channel]).astype(jnp.bfloat16)
            weighted.append(weight.astype(jnp.float32))
        dep_ref[...] += found
        total = grad_ref[...]
        for k in range(step):
            total = total + jac_ref[index * step + k].astype(jnp.float32) * weighted[k]
        grad_ref[...] = total
        return carry

    lax.fori_loop(0, channels // step, some, 0)


def sounding_step(jacobian, columns, innovation, inv_error):
    count, channels, width = jacobian.shape
    rows = 16
    step = next(n for n in (10, 8, 6, 5, 4, 3, 2, 1) if channels % n == 0)
    padded = lane_tiles(channels) * 128
    innovation = jnp.pad(innovation, ((0, 0), (0, padded - channels)))
    departures, grad = pl.pallas_call(
        functools.partial(sounding_kernel, channels, step),
        grid=(count // rows,),
        in_specs=[
            pl.BlockSpec((channels, rows, width), lambda i: (0, i, 0)),
            pl.BlockSpec((rows, width), lambda i: (i, 0)),
            pl.BlockSpec((rows, padded), lambda i: (i, 0)),
            pl.BlockSpec(memory_space=pltpu.SMEM),
        ],
        out_specs=[
            pl.BlockSpec((rows, padded), lambda i: (i, 0)),
            pl.BlockSpec((rows, width), lambda i: (i, 0)),
        ],
        out_shape=[
            jax.ShapeDtypeStruct((count, padded), jnp.float32),
            jax.ShapeDtypeStruct((count, width), jnp.float32),
        ],
        name="soundings",
    )(jnp.transpose(jacobian, (1, 0, 2)), columns, innovation, inv_error[None, :])
    return departures[:, :channels], grad


def local(control, std_dev, col_dev, col_cell, jacobian, innovation, inv_error):
    width, lat_rows, lon_cols = control.shape
    devices = lax.axis_size("lat") * lax.axis_size("lon")
    sound_count = col_cell.shape[0]
    slots_each = max(2, 2 * sound_count // devices)
    slots = devices * slots_each

    before, after = around(control.astype(jnp.bfloat16), "lat", False)

    target = col_dev[:, 0]
    onehot = (target[:, None] == jnp.arange(devices, dtype=jnp.int32)[None, :]).astype(jnp.int32)
    below = jnp.arange(sound_count)[:, None] > jnp.arange(sound_count)[None, :]
    earlier = jnp.dot(
        below.astype(jnp.bfloat16), onehot.astype(jnp.bfloat16), preferred_element_type=jnp.float32
    ).astype(jnp.int32)
    order_in = jnp.sum(earlier * onehot, axis=1)
    slot = target * slots_each + order_in
    wanted = jnp.zeros((slots,), jnp.int32).at[slot].set(col_cell)
    requested = lax.all_to_all(
        wanted.reshape(devices, slots_each), ("lat", "lon"), split_axis=0, concat_axis=0, tiled=True
    ).reshape(-1)

    cells = jnp.stack([requested, *around(requested, "lat", False)])
    cells = jnp.stack([cells, *around(cells, "lon", True)]).reshape(3, 3, slots)
    shift = jnp.array([0, -1, 1], jnp.int32)
    rows = (cells // lon_cols + lat_rows * shift[None, :, None]).reshape(-1, 1)
    columns_at = (cells % lon_cols + lon_cols * shift[:, None, None]).reshape(-1, 1)
    row_weight = tap_weights((rows - jnp.arange(lat_rows)[None, :]).astype(jnp.float32), LHALF)
    col_weight = tap_weights((columns_at - jnp.arange(lon_cols)[None, :]).astype(jnp.float32), lon_cols // 2)
    spread = (row_weight[:, :, None] * col_weight[:, None, :]).reshape(-1, lat_rows * lon_cols)
    spread_high, spread_low = halves(spread)

    increment = smooth(control, before, after) * std_dev[:, None, None]
    flat_field = increment.reshape(width, lat_rows * lon_cols)
    picked = jnp.take(flat_field, requested, axis=1).T.astype(jnp.bfloat16)
    returned = lax.all_to_all(
        picked.reshape(devices, slots_each, width), ("lat", "lon"), split_axis=0, concat_axis=0, tiled=True
    )
    columns = returned.reshape(slots, width)[slot]
    departures, column_grad = sounding_step(jacobian, columns, innovation, inv_error)
    outgoing = jnp.zeros((slots, width), jnp.bfloat16).at[slot].set(column_grad.astype(jnp.bfloat16))
    arrived = lax.all_to_all(
        outgoing.reshape(devices, slots_each, width), ("lat", "lon"), split_axis=0, concat_axis=0, tiled=True
    ).reshape(slots, width)
    near = jnp.concatenate([arrived, *around(arrived, "lat", False)], axis=0)
    near = jnp.concatenate([near, *around(near, "lon", True)], axis=0)
    add_up = lambda w: lax.dot_general(
        near, w, (((0,), (0,)), ((), ())), preferred_element_type=jnp.float32
    )
    adjoint = (add_up(spread_high) + add_up(spread_low)) * std_dev[:, None]
    return (departures, increment, adjoint.reshape(width, lat_rows, lon_cols))


def solution(mesh):
    placed = (
        P(None, "lat", "lon"),
        P(),
        P(("lat", "lon"), None),
        P(("lat", "lon")),
        P(("lat", "lon"), None, None),
        P(("lat", "lon"), None),
        P(),
    )
    return jax.shard_map(
        local,
        mesh=mesh,
        in_specs=placed,
        out_specs=(P(("lat", "lon"), None), P(None, "lat", "lon"), P(None, "lat", "lon")),
        check_vma=False,
    )
```

```python
import functools

import jax
import jax.numpy as jnp
from jax import lax
from jax.experimental import pallas as pl
from jax.experimental.pallas import tpu as pltpu
from jax.sharding import PartitionSpec as P

LHALF = 8
HIGHEST = lax.Precision.HIGHEST
MESH = pl.DeviceIdType.MESH


def tap_weights(offset, half_width):
    spread = 2.0 * half_width / 3.0
    taps = jnp.arange(-half_width, half_width + 1, dtype=jnp.int32).astype(jnp.float32)
    norm_total = jnp.sqrt(jnp.sum(jnp.exp(-taps * taps / (spread * spread))))
    weights = jnp.exp(-offset * offset / (2.0 * spread * spread)) / norm_total
    return jnp.where(jnp.abs(offset) <= half_width, weights, jnp.zeros_like(weights))


def band(out_count, in_count, half_width):
    row_index = jnp.arange(out_count, dtype=jnp.int32)[:, None]
    col_index = jnp.arange(in_count, dtype=jnp.int32)[None, :]
    return tap_weights((col_index - row_index - half_width).astype(jnp.float32), half_width)


def shifts(axis, wrap):
    peers = lax.axis_size(axis)
    up = [(i, (i + 1) % peers) for i in range(peers if wrap else peers - 1)]
    return up, [(j, i) for i, j in up]


def around(array, axis, wrap):
    up, down = shifts(axis, wrap)
    return lax.ppermute(array, axis, up), lax.ppermute(array, axis, down)


def halves(weights):
    high = weights.astype(jnp.bfloat16)
    return high, (weights - high.astype(jnp.float32)).astype(jnp.bfloat16)


def dot_split(data, weights):
    high, low = halves(weights)
    dot = lambda w: jnp.dot(data, w, preferred_element_type=jnp.float32)
    return dot(high) + dot(low)


def smooth(field, swapped, far):
    width, lat_rows, lon_cols = field.shape
    extended = jnp.concatenate([swapped.astype(jnp.float32), field, far.astype(jnp.float32)], axis=1)
    lat_band = band(lat_rows, lat_rows + 2 * LHALF, LHALF)
    before, middle, after = lat_band[:, :LHALF], lat_band[:, LHALF:-LHALF], lat_band[:, -LHALF:]
    odd = lax.axis_index("lat") % 2 == 1
    lat_band = jnp.concatenate([jnp.where(odd, before, after), middle, jnp.where(odd, after, before)], axis=1)
    field = jnp.einsum("ij,cjk->cik", lat_band, extended, precision=HIGHEST)
    lon_half, part = lon_cols // 2, width // 2
    rounded = field.astype(jnp.bfloat16)
    paired = lambda piece: jnp.concatenate([piece[:part], piece[part:]], axis=2)
    up, down = shifts("lon", True)
    left = lax.ppermute(paired(rounded[:, :, lon_half:]), "lon", up)
    right = lax.ppermute(paired(rounded[:, :, :lon_half]), "lon", down)
    lon_band = band(lon_cols, lon_cols + 2 * lon_half, lon_half).T
    edge = lambda w: jnp.concatenate(
        [jnp.concatenate([w, jnp.zeros_like(w)], 1), jnp.concatenate([jnp.zeros_like(w), w], 1)], 0
    )
    both = jnp.concatenate([left, right], axis=2).reshape(part * lat_rows, 2 * lon_cols)
    weights = jnp.concatenate([edge(lon_band[:lon_half]), edge(lon_band[-lon_half:])], 0)
    sides = dot_split(both, weights)
    sides = jnp.concatenate([sides[:, :lon_cols], sides[:, lon_cols:]], axis=0)
    own = jnp.dot(
        field.reshape(width * lat_rows, lon_cols), lon_band[lon_half:-lon_half], precision=HIGHEST
    )
    return (own + sides).reshape(width, lat_rows, lon_cols)


def exchange_kernel(
    lat, lon, cuts, tile_ref, wanted_ref, swap_ref, far_ref, requested_ref,
    swap_send, swap_recv, far_send, far_recv, want_send, want_recv,
):
    row, column = lax.axis_index("lat"), lax.axis_index("lon")
    devices, me = lat * lon, row * lon + column
    odd = row % 2
    partner, step = row + 1 - 2 * odd, 2 - 4 * odd
    onward = jnp.logical_and(row + step >= 0, row + step < lat)
    comes = jnp.logical_and(row - step >= 0, row - step < lat)
    place = lambda other: (other // lon, other % lon)

    barrier = pltpu.get_barrier_semaphore()

    def greet(d, carry):
        other = (me + d) % devices
        pl.semaphore_signal(barrier, inc=1, device_id=place(other), device_id_type=MESH)
        return carry

    lax.fori_loop(1, devices, greet, 0)
    pl.semaphore_wait(barrier, devices - 1)

    def request(src, dst, send, recv, other):
        return pltpu.make_async_remote_copy(
            src_ref=wanted_ref.at[src],
            dst_ref=requested_ref.at[dst],
            send_sem=want_send.at[send],
            recv_sem=want_recv.at[recv],
            device_id=place(other),
            device_id_type=MESH,
        )

    def ask(d, carry):
        other = (me + d) % devices
        request(other, me, other, me, other).start()
        return carry

    lax.fori_loop(1, devices, ask, 0)

    def swap(k):
        part = pl.ds(cuts[k], cuts[k + 1] - cuts[k])
        return pltpu.make_async_remote_copy(
            src_ref=tile_ref.at[part],
            dst_ref=swap_ref.at[part],
            send_sem=swap_send.at[k],
            recv_sem=swap_recv.at[k],
            device_id=(partner, column),
            device_id_type=MESH,
        )

    def forward(k):
        part = pl.ds(cuts[k], cuts[k + 1] - cuts[k])
        return pltpu.make_async_remote_copy(
            src_ref=swap_ref.at[part],
            dst_ref=far_ref.at[part],
            send_sem=far_send.at[k],
            recv_sem=far_recv.at[k],
            device_id=(row + step, column),
            device_id_type=MESH,
        )

    pieces = range(len(cuts) - 1)
    for k in pieces:
        swap(k).start()
    requested_ref[me] = wanted_ref[me]

    @pl.when(jnp.logical_not(comes))
    def _():
        far_ref[...] = jnp.zeros_like(far_ref)

    for k in pieces:
        swap(k).wait_recv()

        @pl.when(onward)
        def _():
            forward(k).start()

    def hear(d, carry):
        other = (me + d) % devices
        asked = request(other, other, other, other, other)
        asked.wait_send()
        asked.wait_recv()
        return carry

    lax.fori_loop(1, devices, hear, 0)
    for k in pieces:
        swap(k).wait_send()

        @pl.when(comes)
        def _():
            forward(k).wait_recv()

        @pl.when(onward)
        def _():
            forward(k).wait_send()


def exchange(tile, wanted):
    lat, lon = lax.axis_size("lat"), lax.axis_size("lon")
    devices, slots_each = wanted.shape
    width, pieces = tile.shape[0], 6
    cuts = [width * k // pieces for k in range(pieces + 1)]
    wanted = jnp.pad(wanted, ((0, 0), (0, -slots_each % 128)))[:, None, :]
    vmem = pl.BlockSpec(memory_space=pltpu.VMEM)
    dma = pltpu.SemaphoreType.DMA
    swapped, far, requested = pl.pallas_call(
        functools.partial(exchange_kernel, lat, lon, cuts),
        in_specs=[vmem, vmem],
        out_specs=[vmem, vmem, vmem],
        out_shape=[
            jax.ShapeDtypeStruct(tile.shape, tile.dtype),
            jax.ShapeDtypeStruct(tile.shape, tile.dtype),
            jax.ShapeDtypeStruct(wanted.shape, wanted.dtype),
        ],
        scratch_shapes=[dma((pieces,))] * 4 + [dma((devices,))] * 2,
        compiler_params=pltpu.CompilerParams(collective_id=0, has_side_effects=True),
        name="exchange",
    )(tile, wanted)
    return swapped, far, requested[:, 0, :slots_each]


def lane_tiles(count):
    return -(-count // 128)


def fold_lanes(tile):
    rows, count = tile.shape
    total = tile[:, :128]
    for start in range(128, count, 128):
        total = total + tile[:, start : start + 128]
    return total


def sounding_kernel(channels, step, jac_ref, col_ref, innov_ref, inv_ref, dep_ref, grad_ref):
    rows, width = col_ref.shape
    lanes = lax.broadcasted_iota(jnp.int32, (rows, dep_ref.shape[1]), 1)
    columns = col_ref[...].astype(jnp.float32)
    dep_ref[...] = jnp.zeros_like(dep_ref)
    grad_ref[...] = jnp.zeros_like(grad_ref)

    def some(index, carry):
        weighted = []
        found = jnp.zeros(dep_ref.shape, jnp.float32)
        for k in range(step):
            channel = index * step + k
            product = jac_ref[channel].astype(jnp.float32) * columns
            departure = jnp.sum(product, axis=1, keepdims=True)
            departure = departure - jnp.sum(
                jnp.where(lanes == channel, innov_ref[...], 0.0), axis=1, keepdims=True
            )
            found = found + jnp.where(lanes == channel, departure, 0.0)
            weight = (departure * inv_ref[0, channel]).astype(jnp.bfloat16)
            weighted.append(weight.astype(jnp.float32))
        dep_ref[...] += found
        total = grad_ref[...]
        for k in range(step):
            total = total + jac_ref[index * step + k].astype(jnp.float32) * weighted[k]
        grad_ref[...] = total
        return carry

    lax.fori_loop(0, channels // step, some, 0)


def sounding_step(jacobian, columns, innovation, inv_error):
    count, channels, width = jacobian.shape
    rows = 16
    step = next(n for n in (10, 8, 6, 5, 4, 3, 2, 1) if channels % n == 0)
    padded = lane_tiles(channels) * 128
    innovation = jnp.pad(innovation, ((0, 0), (0, padded - channels)))
    departures, grad = pl.pallas_call(
        functools.partial(sounding_kernel, channels, step),
        grid=(count // rows,),
        in_specs=[
            pl.BlockSpec((channels, rows, width), lambda i: (0, i, 0)),
            pl.BlockSpec((rows, width), lambda i: (i, 0)),
            pl.BlockSpec((rows, padded), lambda i: (i, 0)),
            pl.BlockSpec(memory_space=pltpu.SMEM),
        ],
        out_specs=[
            pl.BlockSpec((rows, padded), lambda i: (i, 0)),
            pl.BlockSpec((rows, width), lambda i: (i, 0)),
        ],
        out_shape=[
            jax.ShapeDtypeStruct((count, padded), jnp.float32),
            jax.ShapeDtypeStruct((count, width), jnp.float32),
        ],
        name="soundings",
    )(jnp.transpose(jacobian, (1, 0, 2)), columns, innovation, inv_error[None, :])
    return departures[:, :channels], grad


def local(control, std_dev, col_dev, col_cell, jacobian, innovation, inv_error):
    width, lat_rows, lon_cols = control.shape
    devices = lax.axis_size("lat") * lax.axis_size("lon")
    sound_count = col_cell.shape[0]
    slots_each = max(2, 2 * sound_count // devices)
    slots = devices * slots_each

    target = col_dev[:, 0]
    onehot = (target[:, None] == jnp.arange(devices, dtype=jnp.int32)[None, :]).astype(jnp.int32)
    below = jnp.arange(sound_count)[:, None] > jnp.arange(sound_count)[None, :]
    earlier = jnp.dot(
        below.astype(jnp.bfloat16), onehot.astype(jnp.bfloat16), preferred_element_type=jnp.float32
    ).astype(jnp.int32)
    order_in = jnp.sum(earlier * onehot, axis=1)
    slot = target * slots_each + order_in
    wanted = jnp.zeros((slots,), jnp.int32).at[slot].set(col_cell)
    swapped, far, requested = exchange(
        control.astype(jnp.bfloat16), wanted.reshape(devices, slots_each)
    )
    requested = requested.reshape(-1)

    cells = jnp.stack([requested, *around(requested, "lat", False)])
    cells = jnp.stack([cells, *around(cells, "lon", True)]).reshape(3, 3, slots)
    shift = jnp.array([0, -1, 1], jnp.int32)
    rows = (cells // lon_cols + lat_rows * shift[None, :, None]).reshape(-1, 1)
    columns_at = (cells % lon_cols + lon_cols * shift[:, None, None]).reshape(-1, 1)
    row_weight = tap_weights((rows - jnp.arange(lat_rows)[None, :]).astype(jnp.float32), LHALF)
    col_weight = tap_weights((columns_at - jnp.arange(lon_cols)[None, :]).astype(jnp.float32), lon_cols // 2)
    spread = (row_weight[:, :, None] * col_weight[:, None, :]).reshape(3, 3 * slots, lat_rows * lon_cols)
    spread_high, spread_low = halves(spread)

    increment = smooth(control, swapped, far) * std_dev[:, None, None]
    flat_field = increment.reshape(width, lat_rows * lon_cols)
    picked = jnp.take(flat_field, requested, axis=1).T.astype(jnp.bfloat16)
    returned = lax.all_to_all(
        picked.reshape(devices, slots_each, width), ("lat", "lon"), split_axis=0, concat_axis=0, tiled=True
    )
    columns = returned.reshape(slots, width)[slot]
    departures, column_grad = sounding_step(jacobian, columns, innovation, inv_error)
    outgoing = jnp.zeros((slots, width), jnp.bfloat16).at[slot].set(column_grad.astype(jnp.bfloat16))
    arrived = lax.all_to_all(
        outgoing.reshape(devices, slots_each, width), ("lat", "lon"), split_axis=0, concat_axis=0, tiled=True
    ).reshape(slots, width)
    near = jnp.concatenate([arrived, *around(arrived, "lat", False)], axis=0)
    adjoint = jnp.zeros((width, lat_rows * lon_cols), jnp.float32)
    for at, grads in enumerate([near, *around(near, "lon", True)]):
        for spread in (spread_high, spread_low):
            adjoint += lax.dot_general(
                grads, spread[at], (((0,), (0,)), ((), ())), preferred_element_type=jnp.float32
            )
    adjoint = adjoint * std_dev[:, None]
    return (departures, increment, adjoint.reshape(width, lat_rows, lon_cols))


def solution(mesh):
    placed = (
        P(None, "lat", "lon"),
        P(),
        P(("lat", "lon"), None),
        P(("lat", "lon")),
        P(("lat", "lon"), None, None),
        P(("lat", "lon"), None),
        P(),
    )
    return jax.shard_map(
        local,
        mesh=mesh,
        in_specs=placed,
        out_specs=(P(("lat", "lon"), None), P(None, "lat", "lon"), P(None, "lat", "lon")),
        check_vma=False,
    )
```

```python
import functools

import jax
import jax.numpy as jnp
from jax import lax
from jax.experimental import pallas as pl
from jax.experimental.pallas import tpu as pltpu
from jax.sharding import PartitionSpec as P

LHALF = 8
HIGHEST = lax.Precision.HIGHEST
MESH = pl.DeviceIdType.MESH


def tap_weights(offset, half_width):
    spread = 2.0 * half_width / 3.0
    taps = jnp.arange(-half_width, half_width + 1, dtype=jnp.int32).astype(jnp.float32)
    norm_total = jnp.sqrt(jnp.sum(jnp.exp(-taps * taps / (spread * spread))))
    weights = jnp.exp(-offset * offset / (2.0 * spread * spread)) / norm_total
    return jnp.where(jnp.abs(offset) <= half_width, weights, jnp.zeros_like(weights))


def band(out_count, in_count, half_width):
    row_index = jnp.arange(out_count, dtype=jnp.int32)[:, None]
    col_index = jnp.arange(in_count, dtype=jnp.int32)[None, :]
    return tap_weights((col_index - row_index - half_width).astype(jnp.float32), half_width)


def shifts(axis, wrap):
    peers = lax.axis_size(axis)
    up = [(i, (i + 1) % peers) for i in range(peers if wrap else peers - 1)]
    return up, [(j, i) for i, j in up]


def around(array, axis, wrap):
    up, down = shifts(axis, wrap)
    return lax.ppermute(array, axis, up), lax.ppermute(array, axis, down)


def halves(weights):
    high = weights.astype(jnp.bfloat16)
    return high, (weights - high.astype(jnp.float32)).astype(jnp.bfloat16)


def dot_split(data, weights):
    high, low = halves(weights)
    dot = lambda w: jnp.dot(data, w, preferred_element_type=jnp.float32)
    return dot(high) + dot(low)


def smooth(field, swapped, far):
    width, lat_rows, lon_cols = field.shape
    extended = jnp.concatenate([swapped.astype(jnp.float32), field, far.astype(jnp.float32)], axis=1)
    lat_band = band(lat_rows, lat_rows + 2 * LHALF, LHALF)
    before, middle, after = lat_band[:, :LHALF], lat_band[:, LHALF:-LHALF], lat_band[:, -LHALF:]
    odd = lax.axis_index("lat") % 2 == 1
    lat_band = jnp.concatenate([jnp.where(odd, before, after), middle, jnp.where(odd, after, before)], axis=1)
    field = jnp.einsum("ij,cjk->cik", lat_band, extended, precision=HIGHEST)
    lon_half, part = lon_cols // 2, width // 2
    rounded = field.astype(jnp.bfloat16)
    paired = lambda piece: jnp.concatenate([piece[:part], piece[part:]], axis=2)
    up, down = shifts("lon", True)
    left = lax.ppermute(paired(rounded[:, :, lon_half:]), "lon", up)
    right = lax.ppermute(paired(rounded[:, :, :lon_half]), "lon", down)
    lon_band = band(lon_cols, lon_cols + 2 * lon_half, lon_half).T
    edge = lambda w: jnp.concatenate(
        [jnp.concatenate([w, jnp.zeros_like(w)], 1), jnp.concatenate([jnp.zeros_like(w), w], 1)], 0
    )
    both = jnp.concatenate([left, right], axis=2).reshape(part * lat_rows, 2 * lon_cols)
    weights = jnp.concatenate([edge(lon_band[:lon_half]), edge(lon_band[-lon_half:])], 0)
    sides = dot_split(both, weights)
    sides = jnp.concatenate([sides[:, :lon_cols], sides[:, lon_cols:]], axis=0)
    own = jnp.dot(
        field.reshape(width * lat_rows, lon_cols), lon_band[lon_half:-lon_half], precision=HIGHEST
    )
    return (own + sides).reshape(width, lat_rows, lon_cols)


def exchange_kernel(
    lat, lon, cuts, tile_ref, wanted_ref, swap_ref, far_ref, requested_ref,
    swap_send, swap_recv, far_send, far_recv, want_send, want_recv,
):
    row, column = lax.axis_index("lat"), lax.axis_index("lon")
    devices, me = lat * lon, row * lon + column
    odd = row % 2
    partner, step = row + 1 - 2 * odd, 2 - 4 * odd
    onward = jnp.logical_and(row + step >= 0, row + step < lat)
    comes = jnp.logical_and(row - step >= 0, row - step < lat)
    place = lambda other: (other // lon, other % lon)

    barrier = pltpu.get_barrier_semaphore()

    def greet(d, carry):
        other = (me + d) % devices
        pl.semaphore_signal(barrier, inc=1, device_id=place(other), device_id_type=MESH)
        return carry

    lax.fori_loop(1, devices, greet, 0)
    pl.semaphore_wait(barrier, devices - 1)

    def request(dst, send, recv, other):
        return pltpu.make_async_remote_copy(
            src_ref=wanted_ref.at[0],
            dst_ref=requested_ref.at[dst],
            send_sem=want_send.at[send],
            recv_sem=want_recv.at[recv],
            device_id=place(other),
            device_id_type=MESH,
        )

    def ask(d, carry):
        other = (me + d) % devices
        request(me, other, me, other).start()
        return carry

    lax.fori_loop(1, devices, ask, 0)

    def swap(k):
        part = pl.ds(cuts[k], cuts[k + 1] - cuts[k])
        return pltpu.make_async_remote_copy(
            src_ref=tile_ref.at[part],
            dst_ref=swap_ref.at[part],
            send_sem=swap_send.at[k],
            recv_sem=swap_recv.at[k],
            device_id=(partner, column),
            device_id_type=MESH,
        )

    def forward(k):
        part = pl.ds(cuts[k], cuts[k + 1] - cuts[k])
        return pltpu.make_async_remote_copy(
            src_ref=swap_ref.at[part],
            dst_ref=far_ref.at[part],
            send_sem=far_send.at[k],
            recv_sem=far_recv.at[k],
            device_id=(row + step, column),
            device_id_type=MESH,
        )

    pieces = range(len(cuts) - 1)
    for k in pieces:
        swap(k).start()
    requested_ref[me] = wanted_ref[0]

    @pl.when(jnp.logical_not(comes))
    def _():
        far_ref[...] = jnp.zeros_like(far_ref)

    for k in pieces:
        swap(k).wait_recv()

        @pl.when(onward)
        def _():
            forward(k).start()

    def hear(d, carry):
        other = (me + d) % devices
        asked = request(other, other, other, other)
        asked.wait_send()
        asked.wait_recv()
        return carry

    lax.fori_loop(1, devices, hear, 0)
    for k in pieces:
        swap(k).wait_send()

        @pl.when(comes)
        def _():
            forward(k).wait_recv()

        @pl.when(onward)
        def _():
            forward(k).wait_send()


def exchange(tile, wanted):
    lat, lon = lax.axis_size("lat"), lax.axis_size("lon")
    devices, slots = lat * lon, wanted.shape[0]
    width, pieces = tile.shape[0], 6
    cuts = [width * k // pieces for k in range(pieces + 1)]
    wanted = jnp.pad(wanted, (0, -slots % 128))[None, None, :]
    vmem = pl.BlockSpec(memory_space=pltpu.VMEM)
    dma = pltpu.SemaphoreType.DMA
    swapped, far, requested = pl.pallas_call(
        functools.partial(exchange_kernel, lat, lon, cuts),
        in_specs=[vmem, vmem],
        out_specs=[vmem, vmem, vmem],
        out_shape=[
            jax.ShapeDtypeStruct(tile.shape, tile.dtype),
            jax.ShapeDtypeStruct(tile.shape, tile.dtype),
            jax.ShapeDtypeStruct((devices, *wanted.shape[1:]), wanted.dtype),
        ],
        scratch_shapes=[dma((pieces,))] * 4 + [dma((devices,))] * 2,
        compiler_params=pltpu.CompilerParams(collective_id=0, has_side_effects=True),
        name="exchange",
    )(tile, wanted)
    return swapped, far, requested[:, 0, :slots]


def lane_tiles(count):
    return -(-count // 128)


def fold_lanes(tile):
    rows, count = tile.shape
    total = tile[:, :128]
    for start in range(128, count, 128):
        total = total + tile[:, start : start + 128]
    return total


def sounding_kernel(channels, step, jac_ref, col_ref, innov_ref, inv_ref, dep_ref, grad_ref):
    rows, width = col_ref.shape
    lanes = lax.broadcasted_iota(jnp.int32, (rows, dep_ref.shape[1]), 1)
    columns = col_ref[...].astype(jnp.float32)
    dep_ref[...] = jnp.zeros_like(dep_ref)
    grad_ref[...] = jnp.zeros_like(grad_ref)

    def some(index, carry):
        weighted = []
        found = jnp.zeros(dep_ref.shape, jnp.float32)
        for k in range(step):
            channel = index * step + k
            product = jac_ref[channel].astype(jnp.float32) * columns
            departure = jnp.sum(product, axis=1, keepdims=True)
            departure = departure - jnp.sum(
                jnp.where(lanes == channel, innov_ref[...], 0.0), axis=1, keepdims=True
            )
            found = found + jnp.where(lanes == channel, departure, 0.0)
            weight = (departure * inv_ref[0, channel]).astype(jnp.bfloat16)
            weighted.append(weight.astype(jnp.float32))
        dep_ref[...] += found
        total = grad_ref[...]
        for k in range(step):
            total = total + jac_ref[index * step + k].astype(jnp.float32) * weighted[k]
        grad_ref[...] = total
        return carry

    lax.fori_loop(0, channels // step, some, 0)


def sounding_step(jacobian, columns, innovation, inv_error):
    count, channels, width = jacobian.shape
    rows = 16
    step = next(n for n in (10, 8, 6, 5, 4, 3, 2, 1) if channels % n == 0)
    padded = lane_tiles(channels) * 128
    innovation = jnp.pad(innovation, ((0, 0), (0, padded - channels)))
    departures, grad = pl.pallas_call(
        functools.partial(sounding_kernel, channels, step),
        grid=(count // rows,),
        in_specs=[
            pl.BlockSpec((channels, rows, width), lambda i: (0, i, 0)),
            pl.BlockSpec((rows, width), lambda i: (i, 0)),
            pl.BlockSpec((rows, padded), lambda i: (i, 0)),
            pl.BlockSpec(memory_space=pltpu.SMEM),
        ],
        out_specs=[
            pl.BlockSpec((rows, padded), lambda i: (i, 0)),
            pl.BlockSpec((rows, width), lambda i: (i, 0)),
        ],
        out_shape=[
            jax.ShapeDtypeStruct((count, padded), jnp.float32),
            jax.ShapeDtypeStruct((count, width), jnp.float32),
        ],
        name="soundings",
    )(jnp.transpose(jacobian, (1, 0, 2)), columns, innovation, inv_error[None, :])
    return departures[:, :channels], grad


def adjoint_kernel(near_ref, before_ref, after_ref, col_ref, row_ref, std_ref, out_ref):
    lon_cols = col_ref.shape[1]
    total = jnp.zeros((2 * lon_cols, near_ref.shape[1]), jnp.float32)
    for at, grads in enumerate((near_ref, before_ref, after_ref)):
        high, low = halves(col_ref[at] * row_ref[0, at])
        both = jnp.concatenate([high, low], axis=0)
        total = total + jnp.dot(both, grads[...], preferred_element_type=jnp.float32)
    total = (total[:lon_cols] + total[lon_cols:]) * std_ref[...]
    out_ref[...] = total.T


def adjoint_step(grads, rows, columns_at, std_dev, lat_rows, lon_cols):
    slots, width = grads[0].shape
    down = jnp.arange(lat_rows)[:, None, None, None]
    row_weight = tap_weights((rows[None, :, None, :] - down).astype(jnp.float32), LHALF)
    along = jnp.arange(lon_cols)[None, :, None]
    col_weight = tap_weights((columns_at[:, None, :] - along).astype(jnp.float32), lon_cols // 2)
    whole = pl.BlockSpec((slots, width), lambda i: (0, 0))
    return pl.pallas_call(
        adjoint_kernel,
        grid=(lat_rows,),
        in_specs=[
            whole,
            whole,
            whole,
            pl.BlockSpec((3, lon_cols, slots), lambda i: (0, 0, 0)),
            pl.BlockSpec((1, 3, 1, slots), lambda i: (i, 0, 0, 0)),
            pl.BlockSpec((1, width), lambda i: (0, 0)),
        ],
        out_specs=pl.BlockSpec((width, lon_cols), lambda i: (0, i)),
        out_shape=jax.ShapeDtypeStruct((width, lat_rows * lon_cols), jnp.float32),
        name="adjoint",
    )(*grads, col_weight, row_weight, std_dev[None, :])


def local(control, std_dev, col_dev, col_cell, jacobian, innovation, inv_error):
    width, lat_rows, lon_cols = control.shape
    devices = lax.axis_size("lat") * lax.axis_size("lon")
    sound_count = col_cell.shape[0]
    slots_each = max(2, 2 * sound_count // devices)
    slots = devices * slots_each

    target = col_dev[:, 0]
    onehot = (target[:, None] == jnp.arange(devices, dtype=jnp.int32)[None, :]).astype(jnp.int32)
    below = jnp.arange(sound_count)[:, None] > jnp.arange(sound_count)[None, :]
    earlier = jnp.dot(
        below.astype(jnp.bfloat16), onehot.astype(jnp.bfloat16), preferred_element_type=jnp.float32
    ).astype(jnp.int32)
    order_in = jnp.sum(earlier * onehot, axis=1)
    slot = target * slots_each + order_in
    wanted = jnp.zeros((slots,), jnp.int32).at[slot].set(col_cell)
    swapped, far, table = exchange(control.astype(jnp.bfloat16), wanted)
    lat_at, lon_at = lax.axis_index("lat"), lax.axis_index("lon")
    lat_devices, lon_devices = lax.axis_size("lat"), lax.axis_size("lon")

    def asked_of(lat_shift, lon_shift):
        row = jnp.clip(lat_at + lat_shift, 0, lat_devices - 1)
        owner = row * lon_devices + (lon_at + lon_shift) % lon_devices
        return lax.dynamic_slice(table, (0, owner * slots_each), (devices, slots_each))

    requested = asked_of(0, 0).reshape(-1)

    increment = smooth(control, swapped, far) * std_dev[:, None, None]
    flat_field = increment.reshape(width, lat_rows * lon_cols)
    picked = jnp.take(flat_field, requested, axis=1).T.astype(jnp.bfloat16)
    returned = lax.all_to_all(
        picked.reshape(devices, slots_each, width), ("lat", "lon"), split_axis=0, concat_axis=0, tiled=True
    )
    columns = returned.reshape(slots, width)[slot]
    departures, column_grad = sounding_step(jacobian, columns, innovation, inv_error)
    outgoing = jnp.zeros((slots, width), jnp.bfloat16).at[slot].set(column_grad.astype(jnp.bfloat16))
    arrived = lax.all_to_all(
        outgoing.reshape(devices, slots_each, width), ("lat", "lon"), split_axis=0, concat_axis=0, tiled=True
    ).reshape(slots, width)
    near = jnp.concatenate([arrived, *around(arrived, "lat", False)], axis=0)
    grads = (near, *around(near, "lon", True))
    order = (0, -1, 1)
    cells = jnp.stack([jnp.stack([asked_of(up, along) for up in order]) for along in order])
    cells = cells.reshape(3, 3, slots)
    shift = jnp.array(order, jnp.int32)
    rows = (cells // lon_cols + lat_rows * shift[None, :, None]).reshape(3, 3 * slots)
    columns_at = (cells % lon_cols + lon_cols * shift[:, None, None]).reshape(3, 3 * slots)
    adjoint = adjoint_step(grads, rows, columns_at, std_dev, lat_rows, lon_cols)
    return (departures, increment, adjoint.reshape(width, lat_rows, lon_cols))


def solution(mesh):
    placed = (
        P(None, "lat", "lon"),
        P(),
        P(("lat", "lon"), None),
        P(("lat", "lon")),
        P(("lat", "lon"), None, None),
        P(("lat", "lon"), None),
        P(),
    )
    return jax.shard_map(
        local,
        mesh=mesh,
        in_specs=placed,
        out_specs=(P(("lat", "lon"), None), P(None, "lat", "lon"), P(None, "lat", "lon")),
        check_vma=False,
    )
```

```python
import functools

import jax
import jax.numpy as jnp
from jax import lax
from jax.experimental import pallas as pl
from jax.experimental.pallas import tpu as pltpu
from jax.sharding import PartitionSpec as P

LHALF = 8
HIGHEST = lax.Precision.HIGHEST
MESH = pl.DeviceIdType.MESH


def tap_weights(offset, half_width):
    spread = 2.0 * half_width / 3.0
    taps = jnp.arange(-half_width, half_width + 1, dtype=jnp.int32).astype(jnp.float32)
    norm_total = jnp.sqrt(jnp.sum(jnp.exp(-taps * taps / (spread * spread))))
    weights = jnp.exp(-offset * offset / (2.0 * spread * spread)) / norm_total
    return jnp.where(jnp.abs(offset) <= half_width, weights, jnp.zeros_like(weights))


def band(out_count, in_count, half_width):
    row_index = jnp.arange(out_count, dtype=jnp.int32)[:, None]
    col_index = jnp.arange(in_count, dtype=jnp.int32)[None, :]
    return tap_weights((col_index - row_index - half_width).astype(jnp.float32), half_width)


def shifts(axis, wrap):
    peers = lax.axis_size(axis)
    up = [(i, (i + 1) % peers) for i in range(peers if wrap else peers - 1)]
    return up, [(j, i) for i, j in up]


def around(array, axis, wrap):
    up, down = shifts(axis, wrap)
    return lax.ppermute(array, axis, up), lax.ppermute(array, axis, down)


def halves(weights):
    high = weights.astype(jnp.bfloat16)
    return high, (weights - high.astype(jnp.float32)).astype(jnp.bfloat16)


def dot_split(data, weights):
    high, low = halves(weights)
    dot = lambda w: jnp.dot(data, w, preferred_element_type=jnp.float32)
    return dot(high) + dot(low)


def smooth(field, swapped, far):
    width, lat_rows, lon_cols = field.shape
    extended = jnp.concatenate([swapped.astype(jnp.float32), field, far.astype(jnp.float32)], axis=1)
    lat_band = band(lat_rows, lat_rows + 2 * LHALF, LHALF)
    before, middle, after = lat_band[:, :LHALF], lat_band[:, LHALF:-LHALF], lat_band[:, -LHALF:]
    odd = lax.axis_index("lat") % 2 == 1
    lat_band = jnp.concatenate([jnp.where(odd, before, after), middle, jnp.where(odd, after, before)], axis=1)
    field = jnp.einsum("ij,cjk->cik", lat_band, extended, precision=HIGHEST)
    lon_half, part = lon_cols // 2, width // 2
    rounded = field.astype(jnp.bfloat16)
    paired = lambda piece: jnp.concatenate([piece[:part], piece[part:]], axis=2)
    up, down = shifts("lon", True)
    left = lax.ppermute(paired(rounded[:, :, lon_half:]), "lon", up)
    right = lax.ppermute(paired(rounded[:, :, :lon_half]), "lon", down)
    lon_band = band(lon_cols, lon_cols + 2 * lon_half, lon_half).T
    edge = lambda w: jnp.concatenate(
        [jnp.concatenate([w, jnp.zeros_like(w)], 1), jnp.concatenate([jnp.zeros_like(w), w], 1)], 0
    )
    both = jnp.concatenate([left, right], axis=2).reshape(part * lat_rows, 2 * lon_cols)
    weights = jnp.concatenate([edge(lon_band[:lon_half]), edge(lon_band[-lon_half:])], 0)
    sides = dot_split(both, weights)
    sides = jnp.concatenate([sides[:, :lon_cols], sides[:, lon_cols:]], axis=0)
    own = jnp.dot(
        field.reshape(width * lat_rows, lon_cols), lon_band[lon_half:-lon_half], precision=HIGHEST
    )
    return (own + sides).reshape(width, lat_rows, lon_cols)


def exchange_kernel(
    lat, lon, cuts, tile_ref, wanted_ref, swap_ref, far_ref, requested_ref,
    swap_send, swap_recv, far_send, far_recv, want_send, want_recv,
):
    row, column = lax.axis_index("lat"), lax.axis_index("lon")
    devices, me = lat * lon, row * lon + column
    odd = row % 2
    partner, step = row + 1 - 2 * odd, 2 - 4 * odd
    onward = jnp.logical_and(row + step >= 0, row + step < lat)
    comes = jnp.logical_and(row - step >= 0, row - step < lat)
    place = lambda other: (other // lon, other % lon)

    barrier = pltpu.get_barrier_semaphore()

    def greet(d, carry):
        other = (me + d) % devices
        pl.semaphore_signal(barrier, inc=1, device_id=place(other), device_id_type=MESH)
        return carry

    lax.fori_loop(1, devices, greet, 0)
    pl.semaphore_wait(barrier, devices - 1)

    def request(dst, send, recv, other):
        return pltpu.make_async_remote_copy(
            src_ref=wanted_ref.at[0],
            dst_ref=requested_ref.at[dst],
            send_sem=want_send.at[send],
            recv_sem=want_recv.at[recv],
            device_id=place(other),
            device_id_type=MESH,
        )

    def ask(d, carry):
        other = (me + d) % devices
        request(me, other, me, other).start()
        return carry

    lax.fori_loop(1, devices, ask, 0)

    def swap(k):
        part = pl.ds(cuts[k], cuts[k + 1] - cuts[k])
        return pltpu.make_async_remote_copy(
            src_ref=tile_ref.at[part],
            dst_ref=swap_ref.at[part],
            send_sem=swap_send.at[k],
            recv_sem=swap_recv.at[k],
            device_id=(partner, column),
            device_id_type=MESH,
        )

    def forward(k):
        part = pl.ds(cuts[k], cuts[k + 1] - cuts[k])
        return pltpu.make_async_remote_copy(
            src_ref=swap_ref.at[part],
            dst_ref=far_ref.at[part],
            send_sem=far_send.at[k],
            recv_sem=far_recv.at[k],
            device_id=(row + step, column),
            device_id_type=MESH,
        )

    pieces = range(len(cuts) - 1)
    for k in pieces:
        swap(k).start()
    requested_ref[me] = wanted_ref[0]

    @pl.when(jnp.logical_not(comes))
    def _():
        far_ref[...] = jnp.zeros_like(far_ref)

    for k in pieces:
        swap(k).wait_recv()

        @pl.when(onward)
        def _():
            forward(k).start()

    def hear(d, carry):
        other = (me + d) % devices
        asked = request(other, other, other, other)
        asked.wait_send()
        asked.wait_recv()
        return carry

    lax.fori_loop(1, devices, hear, 0)
    for k in pieces:
        swap(k).wait_send()

        @pl.when(comes)
        def _():
            forward(k).wait_recv()

        @pl.when(onward)
        def _():
            forward(k).wait_send()


def exchange(tile, wanted):
    lat, lon = lax.axis_size("lat"), lax.axis_size("lon")
    devices, slots = lat * lon, wanted.shape[0]
    width, pieces = tile.shape[0], 6
    cuts = [width * k // pieces for k in range(pieces + 1)]
    wanted = jnp.pad(wanted, (0, -slots % 128))[None, None, :]
    vmem = pl.BlockSpec(memory_space=pltpu.VMEM)
    dma = pltpu.SemaphoreType.DMA
    swapped, far, requested = pl.pallas_call(
        functools.partial(exchange_kernel, lat, lon, cuts),
        in_specs=[vmem, vmem],
        out_specs=[vmem, vmem, vmem],
        out_shape=[
            jax.ShapeDtypeStruct(tile.shape, tile.dtype),
            jax.ShapeDtypeStruct(tile.shape, tile.dtype),
            jax.ShapeDtypeStruct((devices, *wanted.shape[1:]), wanted.dtype),
        ],
        scratch_shapes=[dma((pieces,))] * 4 + [dma((devices,))] * 2,
        compiler_params=pltpu.CompilerParams(collective_id=0, has_side_effects=True),
        name="exchange",
    )(tile, wanted)
    return swapped, far, requested[:, 0, :slots]


def lane_tiles(count):
    return -(-count // 128)


def sounding_kernel(channels, step, jac_ref, col_ref, innov_ref, inv_ref, dep_ref, out_ref, grad_ref):
    rows, width = col_ref.shape
    padded = dep_ref.shape[1]
    lanes = lax.broadcasted_iota(jnp.int32, (rows, padded), 1)
    columns = col_ref[...].astype(jnp.float32)
    dep_ref[...] = jnp.zeros_like(dep_ref)
    grad_ref[...] = jnp.zeros_like(grad_ref)

    def some(index, carry):
        weighted = []
        found = jnp.zeros(dep_ref.shape, jnp.float32)
        for k in range(step):
            channel = index * step + k
            product = jac_ref[channel].astype(jnp.float32) * columns
            observed = jnp.where(lanes == channel, innov_ref[...], 0.0)
            product = jnp.concatenate([product[:, :padded] - observed, product[:, padded:]], axis=1)
            departure = jnp.sum(product, axis=1, keepdims=True)
            found = found + jnp.where(lanes == channel, departure, 0.0)
            weight = (departure * inv_ref[0, channel]).astype(jnp.bfloat16)
            weighted.append(weight.astype(jnp.float32))
        dep_ref[...] += found
        total = grad_ref[...]
        for k in range(step):
            total = total + jac_ref[index * step + k].astype(jnp.float32) * weighted[k]
        grad_ref[...] = total
        return carry

    lax.fori_loop(0, channels // step, some, 0)
    out_ref[...] = jnp.zeros_like(out_ref)
    out_ref[:, :width] = grad_ref[...].astype(out_ref.dtype)


def sounding_step(jacobian, columns, innovation, inv_error):
    count, channels, width = jacobian.shape
    rows = 16
    step = next(n for n in (10, 8, 6, 5, 4, 3, 2, 1) if channels % n == 0)
    padded = lane_tiles(channels) * 128
    innovation = jnp.pad(innovation, ((0, 0), (0, padded - channels)))
    departures, grad = pl.pallas_call(
        functools.partial(sounding_kernel, channels, step),
        grid=(count // rows,),
        in_specs=[
            pl.BlockSpec((channels, rows, width), lambda i: (0, i, 0)),
            pl.BlockSpec((rows, width), lambda i: (i, 0)),
            pl.BlockSpec((rows, padded), lambda i: (i, 0)),
            pl.BlockSpec(memory_space=pltpu.SMEM),
        ],
        out_specs=[
            pl.BlockSpec((rows, padded), lambda i: (i, 0)),
            pl.BlockSpec((rows, lane_tiles(width) * 128), lambda i: (i, 0)),
        ],
        out_shape=[
            jax.ShapeDtypeStruct((count, padded), jnp.float32),
            jax.ShapeDtypeStruct((count, lane_tiles(width) * 128), jnp.bfloat16),
        ],
        scratch_shapes=[pltpu.VMEM((rows, width), jnp.float32)],
        name="soundings",
    )(jnp.transpose(jacobian, (1, 0, 2)), columns, innovation, inv_error[None, :])
    return departures[:, :channels], grad


def adjoint_kernel(near_ref, before_ref, after_ref, col_ref, row_ref, std_ref, out_ref):
    lon_cols = col_ref.shape[1]
    total = jnp.zeros((2 * lon_cols, near_ref.shape[1]), jnp.float32)
    for at, grads in enumerate((near_ref, before_ref, after_ref)):
        high, low = halves(col_ref[at] * row_ref[0, at])
        both = jnp.concatenate([high, low], axis=0)
        total = total + jnp.dot(both, grads[...], preferred_element_type=jnp.float32)
    total = (total[:lon_cols] + total[lon_cols:]) * std_ref[...]
    out_ref[...] = total.T[: out_ref.shape[0]]


def adjoint_step(grads, rows, columns_at, std_dev, lat_rows, lon_cols):
    slots, wide = grads[0].shape
    width = std_dev.shape[0]
    std_dev = jnp.pad(std_dev, (0, wide - width))
    down = jnp.arange(lat_rows)[:, None, None, None]
    row_weight = tap_weights((rows[None, :, None, :] - down).astype(jnp.float32), LHALF)
    along = jnp.arange(lon_cols)[None, :, None]
    col_weight = tap_weights((columns_at[:, None, :] - along).astype(jnp.float32), lon_cols // 2)
    whole = pl.BlockSpec((slots, wide), lambda i: (0, 0))
    return pl.pallas_call(
        adjoint_kernel,
        grid=(lat_rows,),
        in_specs=[
            whole,
            whole,
            whole,
            pl.BlockSpec((3, lon_cols, slots), lambda i: (0, 0, 0)),
            pl.BlockSpec((1, 3, 1, slots), lambda i: (i, 0, 0, 0)),
            pl.BlockSpec((1, wide), lambda i: (0, 0)),
        ],
        out_specs=pl.BlockSpec((width, lon_cols), lambda i: (0, i)),
        out_shape=jax.ShapeDtypeStruct((width, lat_rows * lon_cols), jnp.float32),
        name="adjoint",
    )(*grads, col_weight, row_weight, std_dev[None, :])


def local(control, std_dev, col_dev, col_cell, jacobian, innovation, inv_error):
    width, lat_rows, lon_cols = control.shape
    devices = lax.axis_size("lat") * lax.axis_size("lon")
    sound_count = col_cell.shape[0]
    slots_each = max(2, 2 * sound_count // devices)
    slots = devices * slots_each

    target = col_dev[:, 0]
    onehot = (target[:, None] == jnp.arange(devices, dtype=jnp.int32)[None, :]).astype(jnp.int32)
    below = jnp.arange(sound_count)[:, None] > jnp.arange(sound_count)[None, :]
    earlier = jnp.dot(
        below.astype(jnp.bfloat16), onehot.astype(jnp.bfloat16), preferred_element_type=jnp.float32
    ).astype(jnp.int32)
    order_in = jnp.sum(earlier * onehot, axis=1)
    slot = target * slots_each + order_in
    wanted = jnp.zeros((slots,), jnp.int32).at[slot].set(col_cell)
    swapped, far, table = exchange(control.astype(jnp.bfloat16), wanted)
    lat_at, lon_at = lax.axis_index("lat"), lax.axis_index("lon")
    lat_devices, lon_devices = lax.axis_size("lat"), lax.axis_size("lon")

    def asked_of(lat_shift, lon_shift):
        row = jnp.clip(lat_at + lat_shift, 0, lat_devices - 1)
        owner = row * lon_devices + (lon_at + lon_shift) % lon_devices
        return lax.dynamic_slice(table, (0, owner * slots_each), (devices, slots_each))

    requested = asked_of(0, 0).reshape(-1)

    increment = smooth(control, swapped, far) * std_dev[:, None, None]
    flat_field = increment.reshape(width, lat_rows * lon_cols)
    picked = jnp.take(flat_field, requested, axis=1).T.astype(jnp.bfloat16)
    returned = lax.all_to_all(
        picked.reshape(devices, slots_each, width), ("lat", "lon"), split_axis=0, concat_axis=0, tiled=True
    )
    columns = returned.reshape(slots, width)[slot]
    departures, column_grad = sounding_step(jacobian, columns, innovation, inv_error)
    wide = column_grad.shape[1]
    outgoing = jnp.zeros((slots, wide), jnp.bfloat16).at[slot].set(column_grad)
    arrived = lax.all_to_all(
        outgoing.reshape(devices, slots_each, wide), ("lat", "lon"), split_axis=0, concat_axis=0, tiled=True
    ).reshape(slots, wide)
    near = jnp.concatenate([arrived, *around(arrived, "lat", False)], axis=0)
    grads = (near, *around(near, "lon", True))
    order = (0, -1, 1)
    cells = jnp.stack([jnp.stack([asked_of(up, along) for up in order]) for along in order])
    cells = cells.reshape(3, 3, slots)
    shift = jnp.array(order, jnp.int32)
    rows = (cells // lon_cols + lat_rows * shift[None, :, None]).reshape(3, 3 * slots)
    columns_at = (cells % lon_cols + lon_cols * shift[:, None, None]).reshape(3, 3 * slots)
    adjoint = adjoint_step(grads, rows, columns_at, std_dev, lat_rows, lon_cols)
    return (departures, increment, adjoint.reshape(width, lat_rows, lon_cols))


def solution(mesh):
    placed = (
        P(None, "lat", "lon"),
        P(),
        P(("lat", "lon"), None),
        P(("lat", "lon")),
        P(("lat", "lon"), None, None),
        P(("lat", "lon"), None),
        P(),
    )
    return jax.shard_map(
        local,
        mesh=mesh,
        in_specs=placed,
        out_specs=(P(("lat", "lon"), None), P(None, "lat", "lon"), P(None, "lat", "lon")),
        check_vma=False,
    )
```
